32 devices in a mesh: tm: 8 (over y, x, core), strip: 4 (over z).
Axes of the slice: x: 2, y: 2, z: 4, core: 2. Of those that a mesh axis runs over, the one named last changes fastest.
Arguments:
- signal: bfloat16 [2, 16, 16384], P(None, 'strip', 'tm'), may hold values from -5 to 5
Outputs:
- spectrum: bfloat16 [2, 256, 16, 8, 2048], P(None, 'strip', None, 'tm')
The draws below stay inside these ranges and needn't reach their ends.
All inputs are finite; a program needn't handle non-finite values.
Results may differ from the reference program's by a relative error of at most 0.0069.
Values may be sent and summed in bfloat16 or wider, within the bound.
A program may use at most 128 MiB of HBM per device.

```python
import math
import jax
import jax.numpy as jnp
from jax import lax

K = 256
L = 16384
W = 16
NRES = 8
LB = 2048


def shard_levels(rng, shape, pieces, least, high):
    level = 1.0
    for axis_at, parts in pieces:
        draws = jax.random.uniform(jax.random.fold_in(jax.random.fold_in(rng, 6), axis_at), (parts,), jnp.float32, least / len(pieces), high / len(pieces))
        level = level * jnp.repeat(jnp.exp(draws), shape[axis_at] // parts).reshape((-1,) + (1,) * (len(shape) - 1 - axis_at))
    return level


def bell_draw(key, dims, deviation, bound, cuts=(), kind=jnp.bfloat16):
    result = deviation * jax.random.normal(key, dims, jnp.float32)
    if cuts:
        result = result * shard_levels(key, dims, cuts, -0.22, 0.18)
    return jnp.clip(result, -bound, bound).astype(kind)


def setup_inputs(seed: int = 0) -> dict:
    splits = jax.random.split(jax.random.key(seed), 2)
    return {
        "signal": bell_draw(splits[0], (2, W, L), 0.7, 5.0, ((1, 4), (2, 8))),
    }


TWO_PI = 2.0 * math.pi

def channel_filters(channel_ids, length):
    offsets = jnp.arange(length, dtype=jnp.int32)
    phases = channel_ids[:, None] * offsets[None, :] % length
    angles = jnp.float32(TWO_PI) * phases.astype(jnp.float32) / length
    hamming = 0.54 - 0.46 * jnp.cos(jnp.float32(TWO_PI) * offsets.astype(jnp.float32) / length)
    scaled = hamming[None, :] / math.sqrt(length)
    cosine = scaled * jnp.cos(angles)
    sine = scaled * jnp.sin(angles)
    real_rows = jnp.stack([cosine, sine], axis=1)
    imag_rows = jnp.stack([-sine, cosine], axis=1)
    return jnp.concatenate([real_rows, imag_rows], axis=0).astype(jnp.bfloat16)

def dft_pair(first, second, modulus, norm):
    phases = first[:, None] * second[None, :] % modulus
    angles = jnp.float32(TWO_PI) * phases.astype(jnp.float32) / modulus
    return (jnp.cos(angles) * norm, jnp.sin(angles) * norm)

def reference(signal):
    filters = channel_filters(jnp.arange(K, dtype=jnp.int32), K).astype(jnp.float32)
    res_ids = jnp.arange(NRES, dtype=jnp.int32)
    blk_ids = jnp.arange(LB, dtype=jnp.int32)
    small_cos, small_sin = dft_pair(res_ids, res_ids, NRES, 1.0 / math.sqrt(NRES))
    small_cos = small_cos.astype(jnp.bfloat16).astype(jnp.float32)
    small_sin = small_sin.astype(jnp.bfloat16).astype(jnp.float32)
    big_cos, big_sin = dft_pair(blk_ids, blk_ids, LB, 1.0 / math.sqrt(LB))
    big_cos = big_cos.astype(jnp.bfloat16).astype(jnp.float32)
    big_sin = big_sin.astype(jnp.bfloat16).astype(jnp.float32)
    twid_cos, twid_sin = dft_pair(res_ids, blk_ids, L, 1.0)
    high = lax.Precision.HIGHEST

    def one_window(window):
        extended = jnp.concatenate([window, jnp.zeros((2, K), jnp.bfloat16)], axis=1)
        wide = extended.astype(jnp.float32)[:, None, :]
        outcome = lax.conv_general_dilated(wide, filters, (1,), 'VALID', dimension_numbers=('CNH', 'OIH', 'CNH'), precision=high, preferred_element_type=jnp.float32)
        spectra = outcome[:, 0, :L].reshape(2, K, L)
        centered = wide[:, 0, K // 2:K // 2 + L]
        real_part = spectra[0] * centered[0][None, :] + spectra[1] * centered[1][None, :]
        imag_part = spectra[1] * centered[0][None, :] - spectra[0] * centered[1][None, :]
        products = jnp.stack([real_part, imag_part]).astype(jnp.bfloat16)
        products = lax.optimization_barrier(products).astype(jnp.float32).reshape(2, K, NRES, LB)
        section_real = jnp.einsum('qn,knm->kqm', small_cos, products[0], precision=high) + jnp.einsum('qn,knm->kqm', small_sin, products[1], precision=high)
        section_imag = jnp.einsum('qn,knm->kqm', small_cos, products[1], precision=high) - jnp.einsum('qn,knm->kqm', small_sin, products[0], precision=high)
        turned_real = section_real * twid_cos[None] + section_imag * twid_sin[None]
        turned_imag = section_imag * twid_cos[None] - section_real * twid_sin[None]
        partial_sums = jnp.stack([turned_real, turned_imag]).astype(jnp.bfloat16)
        partial_sums = lax.optimization_barrier(partial_sums).astype(jnp.float32)
        out_real = jnp.dot(partial_sums[0], big_cos, precision=high) + jnp.dot(partial_sums[1], big_sin, precision=high)
        out_imag = jnp.dot(partial_sums[1], big_cos, precision=high) - jnp.dot(partial_sums[0], big_sin, precision=high)
        return jnp.stack([out_real, out_imag]).astype(jnp.bfloat16)
    spectra_all = lax.map(one_window, jnp.transpose(signal, (1, 0, 2)))
    return jnp.transpose(spectra_all, (1, 2, 0, 3, 4))
```

```python
import math

import jax
import jax.numpy as jnp
from jax import lax
from jax.experimental import pallas as pl
from jax.experimental.pallas import tpu as pltpu
from jax.sharding import PartitionSpec as P

K = 256
D = 8
EXTRA = 16
TWO_PI = 2.0 * math.pi


def unit_pair(phases, modulus):
    angles = jnp.float32(TWO_PI / modulus) * (phases % modulus).astype(jnp.float32)
    return jnp.cos(angles), jnp.sin(angles)


def channel_filters(channel_ids):
    offsets = jnp.arange(K, dtype=jnp.int32)
    cosine, sine = unit_pair(channel_ids[:, None] * offsets[None, :], K)
    hamming = 0.54 - 0.46 * jnp.cos(jnp.float32(TWO_PI) * offsets.astype(jnp.float32) / K)
    scaled = hamming[None, :] / math.sqrt(K)
    cosine = (scaled * cosine).astype(jnp.bfloat16)
    sine = (scaled * sine).astype(jnp.bfloat16)
    rows = []
    for real_taps, imag_taps in ((cosine, sine), (-sine, cosine)):
        for offset in range(D):
            pad = ((0, 0), (offset, EXTRA - offset))
            rows.append(
                jnp.concatenate([jnp.pad(real_taps, pad), jnp.pad(imag_taps, pad)], axis=1)
            )
    return jnp.concatenate(rows, axis=0)


def small_dft(values):
    count = len(values)
    if count == 1:
        return values
    even = small_dft(values[0::2])
    odd = small_dft(values[1::2])
    low, high = [], []
    for i in range(count // 2):
        er, ei = even[i]
        orr, oi = odd[i]
        if i == 0:
            tr, ti = orr, oi
        elif 4 * i == count:
            tr, ti = oi, -orr
        else:
            c = math.cos(TWO_PI * i / count)
            s = math.sin(TWO_PI * i / count)
            if abs(c - s) < 1e-6:
                tr, ti = (orr + oi) * c, (oi - orr) * c
            elif abs(c + s) < 1e-6:
                tr, ti = (oi - orr) * s, (orr + oi) * (-s)
            else:
                tr, ti = orr * c + oi * s, oi * c - orr * s
        low.append((er + tr, ei + ti))
        high.append((er - tr, ei - ti))
    return low + high


def make_body(blocks, piece, chan):
    total = blocks * piece
    rows = D * chan

    def body(x_ref, filt_ref, turn_ref, dft_ref, twid_ref, out_ref, taps_ref, acc_ref):
        parts = [x_ref[0, a, 0] for a in range(blocks)]
        parts.append(jnp.zeros((2 * D, 128), jnp.bfloat16))
        x = jnp.concatenate(parts, axis=1).astype(jnp.float32)
        width = total + 128
        span = K + EXTRA
        for c in range(2):
            base = x[c * D : (c + 1) * D]
            for q in range(0, span // D, 2):
                pair = []
                for s in (q, q + 1):
                    moved = base if s == 0 else pltpu.roll(base, width - s, 1)
                    pair.append(moved[:, :total])
                taps_ref[c * span + q * D : c * span + (q + 2) * D, :] = jnp.concatenate(
                    pair, axis=0
                ).astype(jnp.bfloat16)
        lag = K // 2 // D
        xr = pltpu.roll(x[:D], width - lag, 1)[:, :total]
        xi = pltpu.roll(x[D:], width - lag, 1)[:, :total]
        tc, ts = turn_ref[0], turn_ref[1]
        zr = xr * tc - xi * ts
        zi = -(xi * tc + xr * ts)
        for a in range(blocks):
            lanes = slice(a * piece, (a + 1) * piece)
            res = jnp.dot(
                filt_ref[...], taps_ref[:, lanes], preferred_element_type=jnp.float32
            )
            for o in range(D):
                r0 = o * chan
                fr = res[r0 : r0 + chan]
                fi = res[rows + r0 : rows + r0 + chan]
                br = zr[o : o + 1, lanes]
                bi = zi[o : o + 1, lanes]
                pr = fr * br - fi * bi
                pi = fr * bi + fi * br
                if a > 0:
                    pr = pr + acc_ref[r0 : r0 + chan]
                    pi = pi + acc_ref[rows + r0 : rows + r0 + chan]
                acc_ref[r0 : r0 + chan] = pr
                acc_ref[rows + r0 : rows + r0 + chan] = pi
        partial = jnp.concatenate(
            [acc_ref[:rows].astype(jnp.bfloat16), acc_ref[rows:].astype(jnp.bfloat16)], axis=1
        )
        inner = jnp.dot(partial, dft_ref[...], preferred_element_type=jnp.float32)
        turned = []
        for o in range(D):
            vr = inner[o * chan : (o + 1) * chan, :piece]
            vi = inner[o * chan : (o + 1) * chan, piece:]
            if o > 0:
                tc = twid_ref[0, o : o + 1]
                ts = twid_ref[1, o : o + 1]
                vr, vi = vr * tc + vi * ts, vi * tc - vr * ts
            turned.append((vr, vi))
        for m, (yr, yi) in enumerate(small_dft(turned)):
            out_ref[0, 0, :, m * piece : (m + 1) * piece] = yr.astype(jnp.bfloat16)
            out_ref[0, 1, :, m * piece : (m + 1) * piece] = yi.astype(jnp.bfloat16)

    return body


def per_device(signal):
    blocks = lax.axis_size("tm")
    strips = lax.axis_size("strip")
    wloc, block_len = signal.shape[1], signal.shape[2]
    windows = wloc * strips
    piece = block_len // D
    chan = K // strips
    total = block_len * blocks
    span = K + EXTRA
    local = signal.reshape(2, wloc, piece, D).transpose(1, 0, 3, 2).reshape(wloc, 2 * D, piece)
    every = lax.all_gather(local, ("strip", "tm"), axis=0, tiled=False)
    every = every.reshape(strips, blocks, wloc, 2 * D, piece)
    channel_ids = lax.axis_index("strip") * chan + jnp.arange(chan, dtype=jnp.int32)
    filters = channel_filters(channel_ids)
    residue = lax.axis_index("tm")
    offs = jnp.arange(D, dtype=jnp.int32)
    samples = offs[:, None] + D * jnp.arange(piece * blocks, dtype=jnp.int32)[None, :]
    turn = jnp.stack(unit_pair(residue * samples, total)) * (1.0 / math.sqrt(blocks))
    ids = jnp.arange(piece, dtype=jnp.int32)
    dc, ds = unit_pair(ids[:, None] * ids[None, :], piece)
    dft = jnp.concatenate(
        [jnp.concatenate([dc, -ds], axis=1), jnp.concatenate([ds, dc], axis=1)], axis=0
    ) * (1.0 / math.sqrt(block_len))
    dft = dft.astype(jnp.bfloat16)
    twid = jnp.stack(unit_pair(offs[:, None] * ids[None, :], block_len))

    fixed = lambda *dims: pl.BlockSpec(dims, lambda w: (0,) * len(dims))
    out = pl.pallas_call(
        make_body(blocks, piece, chan),
        grid=(windows,),
        in_specs=[
            pl.BlockSpec((1, blocks, 1, 2 * D, piece), lambda w: (w // wloc, 0, w % wloc, 0, 0)),
            fixed(2 * D * chan, 2 * span),
            fixed(2, D, piece * blocks),
            fixed(2 * piece, 2 * piece),
            fixed(2, D, piece),
        ],
        out_specs=pl.BlockSpec((1, 2, chan, block_len), lambda w: (w, 0, 0, 0)),
        out_shape=jax.ShapeDtypeStruct((windows, 2, chan, block_len), jnp.bfloat16),
        scratch_shapes=[
            pltpu.VMEM((2 * span, piece * blocks), jnp.bfloat16),
            pltpu.VMEM((2 * D * chan, piece), jnp.float32),
        ],
        compiler_params=pltpu.CompilerParams(
            dimension_semantics=("arbitrary",), vmem_limit_bytes=56 * 1024 * 1024
        ),
        name="strip_windows",
    )(every, filters, turn, dft, twid)
    return out.transpose(1, 2, 0, 3).reshape(2, chan, windows, 1, block_len)


def solution(mesh):
    return jax.shard_map(
        per_device,
        mesh=mesh,
        in_specs=(P(None, "strip", "tm"),),
        out_specs=P(None, "strip", None, "tm", None),
        check_vma=False,
    )
```
